32 devices in a mesh: parts: 2 (over y), dp: 4 (over z), tensor: 4 (over x, core).
Axes of the slice: x: 2, y: 2, z: 4, core: 2. Of those that a mesh axis runs over, the one named last changes fastest.
Arguments:
- prompt_kv: bfloat16 [2, 14336, 8, 128], P(None, ('parts', 'dp'), 'tensor'), parts along dimension 1, may hold values from -12 to 12
- gen_kv: bfloat16 [64, 2, 128, 8, 128], P(('parts', 'dp'), None, None, 'tensor'), parts along dimension 0, may hold values from -17 to 17
- queries: bfloat16 [2, 64, 64, 128], P(None, ('parts', 'dp'), 'tensor'), parts along dimension 1, may hold values from -24 to 24
- new_kv: bfloat16 [2, 2, 64, 8, 128], P(None, None, ('parts', 'dp'), 'tensor'), parts along dimension 2, may hold values from -48 to 48
- ancestors: int32 [64], P(('parts', 'dp')), parts along dimension 0, may hold values from 0 to 31, as said below
- prior_twist: float32 [64], P(('parts', 'dp')), parts along dimension 0, may hold values from -290 to 6
- twist_vec: float32 [64, 128], P('tensor'), may hold values from -1 to 1
Outputs:
- attended: bfloat16 [2, 64, 64, 128], P(None, ('parts', 'dp'), 'tensor'), parts along dimension 1
- log_weights: float32 [64], P(('parts', 'dp')), parts along dimension 0
The draws below stay inside these ranges and needn't reach their ends.
There are 2 independent parts, one for each index of `parts`. The reference program is written for one: setup_inputs(seed, part) draws one part's arguments, and reference() takes and returns one part's arrays. A program takes and returns all parts, laid end to end along the dimension named above; an argument that names none is the same for every part. Nothing has to cross between parts.
Inputs may be any that keep to these rules, and one draw needn't show every extreme that they name: Duplicates are allowed. Among the 8 particles of one device (equal p // 8) at most 4 have ancestors held by one same device (equal ancestors // 8), and every device has exactly 4 from some device.
All inputs are finite; a program needn't handle non-finite values.
Results may differ from the reference program's by a relative error of at most 0.0017.
Values may be sent and summed in bfloat16 or wider, within the bound.
A program may use at most 128 MiB of HBM per device.

```python
import math
import jax
import jax.numpy as jnp
from jax import lax

H = 64
KVH = 8
HD = 128
P_DEV = 8
L_DEV = 1792
G = 128
STEPS = 2
CAP = 4
P_SIZE = 32
L = 7168
N_DP = 4


def joint_draw(base_key):
    group_total = (P_DEV + CAP - 1) // CAP

    def one_device(device_key):
        key_list = jax.random.split(device_key, 5)
        ranking = jax.random.randint(key_list[0], (N_DP,), 0, 65536)
        hot_source = (jax.random.randint(key_list[1], (N_DP,), 0, 8) == 0).astype(jnp.int32)
        scored = (ranking + hot_source * 65536) * N_DP + jnp.arange(N_DP, dtype=jnp.int32)
        ordered = jnp.argsort(-scored)
        places = jnp.arange(P_DEV, dtype=jnp.int32)
        bundle = places // CAP
        coin = jax.random.randint(key_list[2], (P_DEV,), 0, 2)
        moved = ((places >= CAP) & (places % CAP == CAP - 1) & (coin == 1)).astype(jnp.int32)
        source = ordered[bundle + group_total * moved]
        first_draw = jax.random.randint(key_list[3], (P_DEV,), 0, P_DEV)
        second_draw = jax.random.randint(key_list[4], (P_DEV,), 0, P_DEV)
        return (source * P_DEV + jnp.minimum(first_draw, second_draw)).astype(jnp.int32)
    device_keys = jax.random.split(jax.random.fold_in(base_key, 11), N_DP)
    ancestors = jax.vmap(one_device)(device_keys).reshape(-1).astype(jnp.int32)
    query_shape = (STEPS, P_SIZE, H, HD)
    drawn_query = jnp.clip(jax.random.normal(jax.random.fold_in(base_key, 13), query_shape), -6.0, 6.0)
    query = drawn_query
    return (ancestors, drawn_query, query)


def draw_ancestors(key, part):
    return joint_draw(key)[0]


def draw_queries(key, part):
    return joint_draw(key)[2].astype(jnp.bfloat16)


def draw_gen_kv(key, part):
    cache_shape = (P_SIZE, G, KVH, HD)
    key_part = 2.8 * jnp.clip(jax.random.normal(jax.random.fold_in(key, 21), cache_shape), -6.0, 6.0)
    value_part = jnp.clip(jax.random.normal(jax.random.fold_in(key, 22), cache_shape), -6.0, 6.0)
    return jnp.stack([key_part, value_part], axis=1).astype(jnp.bfloat16)


def draw_new_kv(key, part):
    ancestors, drawn_query, query = joint_draw(key)
    group_mean = jnp.mean(drawn_query.reshape(STEPS, P_SIZE, KVH, H // KVH, HD), axis=3)
    token_shape = (STEPS, P_SIZE, KVH, HD)
    noise = jnp.clip(jax.random.normal(jax.random.fold_in(key, 23), token_shape), -6.0, 6.0)
    value_part = jnp.clip(jax.random.normal(jax.random.fold_in(key, 24), token_shape), -6.0, 6.0)
    key_part = 7.0 * group_mean + noise
    return jnp.stack([key_part, value_part], axis=1).astype(jnp.bfloat16)


def draw_prompt_kv(key, part):
    prompt_shape = (L, KVH, HD)
    level = jnp.clip(jax.random.normal(jax.random.fold_in(key, 25), (KVH, HD)), -4.0, 4.0)
    key_part = jnp.clip(jax.random.normal(jax.random.fold_in(key, 26), prompt_shape), -6.0, 6.0)
    value_part = jnp.clip(jax.random.normal(jax.random.fold_in(key, 27), prompt_shape), -6.0, 6.0) + level
    return jnp.stack([key_part, value_part], axis=0).astype(jnp.bfloat16)


def draw_prior_twist(key, part):
    return jnp.clip(jax.random.normal(jax.random.fold_in(key, 28), (P_SIZE,)), -4.0, 4.0).astype(jnp.float32)


def draw_twist_vec(key, part):
    head_place = jnp.arange(H).astype(jnp.float32) / (H - 1)
    rising = 3.0 ** head_place
    drawn = jnp.clip(jax.random.normal(jax.random.fold_in(key, 29), (H, HD)), -6.0, 6.0)
    return (drawn * rising[:, None] / math.sqrt(H * HD)).astype(jnp.float32)


def setup_inputs(seed: int = 0, part: int = 0) -> dict:
    splits = jax.random.split(jax.random.key(seed), 8)
    own_keys = jax.random.split(jax.random.fold_in(splits[7], part), 8)
    prompt_kv = draw_prompt_kv(jax.random.fold_in(jax.random.fold_in(splits[7], part), 71), part)
    gen_kv = draw_gen_kv(jax.random.fold_in(jax.random.fold_in(splits[7], part), 71), part)
    queries = draw_queries(jax.random.fold_in(jax.random.fold_in(splits[7], part), 71), part)
    new_kv = draw_new_kv(jax.random.fold_in(jax.random.fold_in(splits[7], part), 71), part)
    ancestors = draw_ancestors(jax.random.fold_in(jax.random.fold_in(splits[7], part), 71), part)
    prior_twist = draw_prior_twist(jax.random.fold_in(jax.random.fold_in(splits[7], part), 71), part)
    twist_vec = draw_twist_vec(jax.random.fold_in(splits[7], 71), part)
    return {"prompt_kv": prompt_kv, "gen_kv": gen_kv, "queries": queries, "new_kv": new_kv, "ancestors": ancestors, "prior_twist": prior_twist, "twist_vec": twist_vec}


def join_states(left_state, right_state):
    largest = jnp.maximum(left_state[0], right_state[0])
    left_scale = jnp.exp(left_state[0] - largest)
    right_scale = jnp.exp(right_state[0] - largest)
    return (largest, left_state[1] * left_scale + right_state[1] * right_scale, left_state[2] * left_scale[..., None] + right_state[2] * right_scale[..., None])

def block_state(scores, values, pattern):
    largest = lax.optimization_barrier(jnp.max(scores, axis=-1))
    exponent = jnp.exp(scores - largest[..., None])
    weights = lax.optimization_barrier(exponent.astype(jnp.bfloat16)).astype(jnp.float32)
    weighted = jnp.einsum(pattern, weights, values.astype(jnp.float32), precision=lax.Precision.HIGHEST)
    return (largest, lax.optimization_barrier(jnp.sum(exponent, axis=-1)), weighted)

def reference(prompt_kv, gen_kv, queries, new_kv, ancestors, prior_twist, twist_vec):
    step_count, particle_count, head_count, head_size = queries.shape
    kv_count = prompt_kv.shape[2]
    group_size = head_count // kv_count
    scaling = 1.0 / math.sqrt(head_size)
    split_query = queries.astype(jnp.float32).reshape(step_count, particle_count, kv_count, group_size, head_size)
    blocks = jnp.moveaxis(prompt_kv.reshape(2, N_DP, L_DEV, kv_count, head_size), 1, 0)

    def prompt_block(carry, block_kv):
        scores = jnp.einsum('spcgd,kcd->spcgk', split_query, block_kv[0].astype(jnp.float32), precision=lax.Precision.HIGHEST) * scaling
        return (join_states(carry, block_state(scores, block_kv[1], 'spcgk,kcd->spcgd')), None)
    start_shape = (step_count, particle_count, kv_count, group_size)
    initial = (jnp.full(start_shape, -jnp.inf, jnp.float32), jnp.zeros(start_shape, jnp.float32), jnp.zeros(start_shape + (head_size,), jnp.float32))
    prompt_state, _ = lax.scan(prompt_block, initial, blocks)
    resampled = jnp.take(gen_kv, ancestors, axis=0)
    cache_scores = jnp.einsum('spcgd,pkcd->spcgk', split_query, resampled[:, 0].astype(jnp.float32), precision=lax.Precision.HIGHEST) * scaling
    cached = block_state(cache_scores, resampled[:, 1], 'spcgk,pkcd->spcgd')
    new_scores = jnp.einsum('spcgd,tpcd->spcgt', split_query, new_kv[:, 0].astype(jnp.float32), precision=lax.Precision.HIGHEST) * scaling
    positions = jnp.arange(step_count)
    allowed = positions[None, :] <= positions[:, None]
    new_scores = jnp.where(allowed[:, None, None, None, :], new_scores, -jnp.inf)
    fresh_state = block_state(new_scores, new_kv[:, 1], 'spcgt,tpcd->spcgd')
    joined = join_states(join_states(prompt_state, cached), fresh_state)
    attended = (joined[2] / joined[1][..., None]).reshape(step_count, particle_count, head_count, head_size)
    attended = attended.astype(jnp.bfloat16)
    last_step = lax.optimization_barrier(attended[-1]).astype(jnp.float32)
    twist_value = lax.optimization_barrier(jnp.sum(last_step * twist_vec, axis=(1, 2)))
    raw_weight = twist_value - jnp.take(prior_twist, ancestors, axis=0)
    largest = jnp.max(raw_weight)
    normalizer = largest + jnp.log(jnp.sum(jnp.exp(raw_weight - largest)))
    return (attended, raw_weight - normalizer)
```

```python
import functools
import math

import jax
import jax.numpy as jnp
from jax import lax
from jax.experimental import pallas as pl
from jax.experimental.pallas import tpu as pltpu
from jax.sharding import PartitionSpec as P

MESH = pl.DeviceIdType.MESH
MASKED = -1e30
LEVELS = 32767.0


def nt(a, b):
    return lax.dot_general(a, b, (((1,), (1,)), ((), ())), preferred_element_type=jnp.float32)


def tn_dot(a, b):
    return lax.dot_general(a, b, (((0,), (0,)), ((), ())), preferred_element_type=jnp.float32)


def kernel(
    sizes,
    anc_ref,
    prior_ref,
    vec_ref,
    new_ref,
    q_hbm,
    prompt_hbm,
    gen_hbm,
    att_ref,
    lw_ref,
    prompt_buf,
    gen_buf,
    wide,
    keys,
    vals,
    gkeys,
    gvals,
    q_all,
    meta_own,
    meta_all,
    res_send,
    res_recv,
    stat_send,
    stat_recv,
    tens_own,
    tens_all,
    dp_own,
    dp_all,
    local_sem,
    q_ssem,
    q_rsem,
    m_ssem,
    m_rsem,
    r_ssem,
    r_rsem,
    s_ssem,
    s_rsem,
    t_ssem,
    t_rsem,
    d_ssem,
    d_rsem,
):
    devices, tensors, steps, local, kv_count, group, positions, cached, head = sizes
    rows = steps * local * group
    all_heads = kv_count * group
    me = lax.axis_index("dp")
    mine = lax.axis_index("tensor")
    factor = math.log2(math.e) / math.sqrt(head)

    def remote(src, dst, ssem, rsem, **where):
        return pltpu.make_async_remote_copy(
            src_ref=src, dst_ref=dst, send_sem=ssem, recv_sem=rsem,
            device_id=where, device_id_type=MESH,
        )

    barrier = pltpu.get_barrier_semaphore()

    @pl.loop(1, devices)
    def _(k):
        pl.semaphore_signal(
            barrier, inc=1, device_id={"dp": lax.rem(me + k, devices)}, device_id_type=MESH
        )

    @pl.loop(1, tensors)
    def _(k):
        pl.semaphore_signal(
            barrier, inc=1, device_id={"tensor": lax.rem(mine + k, tensors)}, device_id_type=MESH
        )

    copy_q = pltpu.make_async_copy(q_hbm, q_all.at[me], local_sem.at[0])
    copy_q.start()
    copy_k = pltpu.make_async_copy(prompt_hbm.at[0], prompt_buf.at[0], local_sem.at[1])
    copy_k.start()
    copy_v = pltpu.make_async_copy(prompt_hbm.at[1], prompt_buf.at[1], local_sem.at[2])
    copy_v.start()
    copy_g = pltpu.make_async_copy(gen_hbm, gen_buf, local_sem.at[3])
    copy_g.start()

    lane = lax.broadcasted_iota(jnp.int32, (8, rows), 1)
    sub = lax.broadcasted_iota(jnp.int32, (8, rows), 0)
    lane_particle = lax.rem(lax.div(lane, group), local)
    meta = jnp.zeros((8, rows), jnp.float32)
    for j in range(local):
        meta = jnp.where(
            (sub == 0) & (lane_particle == j), anc_ref[j].astype(jnp.float32), meta
        )
        meta = jnp.where((sub == 1) & (lane == j), prior_ref[j], meta)
    meta_own[...] = meta
    meta_all[me] = meta

    pl.semaphore_wait(barrier, devices - 1 + tensors - 1)

    def q_copy(peer, slot):
        return remote(q_hbm, q_all.at[slot], q_ssem.at[peer], q_rsem.at[slot], dp=peer)

    def m_copy(peer, slot):
        return remote(meta_own, meta_all.at[slot], m_ssem.at[peer], m_rsem.at[slot], dp=peer)

    def r_copy(peer, slot):
        return remote(res_send.at[peer], res_recv.at[slot], r_ssem.at[peer], r_rsem.at[slot], dp=peer)

    def s_copy(peer, slot):
        return remote(stat_send.at[peer], stat_recv.at[slot], s_ssem.at[peer], s_rsem.at[slot], dp=peer)

    @pl.loop(1, devices)
    def _(k):
        peer = lax.rem(me + k, devices)
        m_copy(peer, me).start()
        q_copy(peer, me).start()

    def split(source, count):
        wide[pl.ds(0, count * kv_count), :] = source.astype(jnp.float32)
        return [
            wide[pl.ds(c, count, stride=kv_count), :] if kv_count > 1 else wide[pl.ds(0, count), :]
            for c in range(kv_count)
        ]

    chunk = cached

    copy_k.wait()

    @pl.loop(0, positions // chunk)
    def _(i):
        at = pl.ds(pl.multiple_of(i * (chunk * kv_count), chunk * kv_count), chunk * kv_count)
        for c, part in enumerate(split(prompt_buf[0, at, :], chunk)):
            keys[c, pl.ds(pl.multiple_of(i * chunk, chunk), chunk), :] = part.astype(jnp.bfloat16)

    copy_v.wait()

    @pl.loop(0, positions // chunk)
    def _(i):
        at = pl.ds(pl.multiple_of(i * (chunk * kv_count), chunk * kv_count), chunk * kv_count)
        for c, part in enumerate(split(prompt_buf[1, at, :], chunk)):
            vals[c, :, pl.ds(pl.multiple_of(i * chunk, chunk), chunk)] = part.T.astype(jnp.bfloat16)

    copy_g.wait()

    @pl.loop(0, local)
    def _(i):
        at = pl.ds(pl.multiple_of(i * chunk, chunk), chunk)
        for c, part in enumerate(split(gen_buf[i, 0], chunk)):
            gkeys[c, at, :] = part.astype(jnp.bfloat16)
        for c, part in enumerate(split(gen_buf[i, 1], chunk)):
            gvals[c, :, at] = part.T.astype(jnp.bfloat16)

    def rows_of(slot, c):
        q = q_all[slot].astype(jnp.float32).reshape(steps * local, kv_count, group, head)
        return q[:, c].reshape(rows, head).astype(jnp.bfloat16)

    def partial(slot, res, stat):
        ancestor = meta_all[slot, 0:1, :]
        held = (ancestor - (me * local).astype(jnp.float32)).astype(jnp.int32)
        for c in range(kv_count):
            q = rows_of(slot, c)
            score = nt(keys[c], q)
            top = jnp.max(score, axis=0, keepdims=True)
            weight = jnp.exp2((score - top) * factor)
            total = jnp.sum(weight, axis=0, keepdims=True)
            value = jnp.dot(vals[c], weight.astype(jnp.bfloat16), preferred_element_type=jnp.float32)
            gscore = nt(gkeys[c], q).reshape(local, cached, rows)
            which = lax.broadcasted_iota(jnp.int32, (local, 1, rows), 0)
            gscore = jnp.where(which == held[None], gscore, MASKED).reshape(local * cached, rows)
            gtop = jnp.max(gscore, axis=0, keepdims=True)
            gweight = jnp.exp2((gscore - gtop) * factor)
            gtotal = jnp.sum(gweight, axis=0, keepdims=True)
            gvalue = jnp.dot(gvals[c], gweight.astype(jnp.bfloat16), preferred_element_type=jnp.float32)
            both = jnp.maximum(top, gtop)
            one = jnp.exp2((top - both) * factor)
            two = jnp.exp2((gtop - both) * factor)
            value = value * one + gvalue * two
            total = total * one + gtotal * two
            largest = jnp.maximum(jnp.max(jnp.abs(value), axis=0, keepdims=True), 1e-30)
            coded = value * (LEVELS / largest)
            coded = coded + jnp.where(coded >= 0, 0.5, -0.5)
            res[c] = coded.astype(jnp.int32).astype(jnp.int16)
            stat[c, 0:1, :] = both
            stat[c, 1:2, :] = total
            stat[c, 2:3, :] = largest * (1.0 / LEVELS)

    copy_q.wait()
    partial(me, res_recv.at[me], stat_recv.at[me])

    @pl.loop(1, devices)
    def _(k):
        peer = lax.rem(me + devices - k, devices)
        m_copy(peer, peer).wait_recv()
        q_copy(peer, peer).wait_recv()
        partial(peer, res_send.at[peer], stat_send.at[peer])
        s_copy(peer, me).start()
        r_copy(peer, me).start()

    fresh_keys = jnp.concatenate(
        [new_ref[t, 0].astype(jnp.float32) for t in range(steps)], axis=0
    ).astype(jnp.bfloat16)
    fresh_vals = jnp.concatenate(
        [new_ref[t, 1].astype(jnp.float32) for t in range(steps)], axis=0
    ).astype(jnp.bfloat16)
    count = steps * local * kv_count
    key_place = lax.broadcasted_iota(jnp.int32, (count, rows), 0)
    row_place = lax.broadcasted_iota(jnp.int32, (count, rows), 1)
    key_head = lax.rem(key_place, kv_count)
    key_particle = lax.rem(lax.div(key_place, kv_count), local)
    key_step = lax.div(key_place, kv_count * local)
    row_particle = lax.rem(lax.div(row_place, group), local)
    row_step = lax.div(row_place, group * local)
    fits = (key_particle == row_particle) & (key_step <= row_step)
    fresh = []
    for c in range(kv_count):
        score = jnp.where(fits & (key_head == c), nt(fresh_keys, rows_of(me, c)), MASKED)
        top = jnp.max(score, axis=0, keepdims=True)
        weight = jnp.exp2((score - top) * factor)
        total = jnp.sum(weight, axis=0, keepdims=True)
        fresh.append((top, total, tn_dot(fresh_vals, weight.astype(jnp.bfloat16))))

    lane8 = lax.broadcasted_iota(jnp.int32, (local, head), 1)
    sub8 = lax.broadcasted_iota(jnp.int32, (local, head), 0)
    own_ancestor = jnp.zeros((local, head), jnp.int32)
    for j in range(local):
        own_ancestor = jnp.where(sub8 == j, anc_ref[j], own_ancestor)

    def add_before(i, before):
        prior = meta_all[i, 1:2, :]
        hit = (own_ancestor - i * local == lane8) & (lane8 < local)
        return before + jnp.where(hit, prior, 0.0)

    before = lax.fori_loop(0, devices, add_before, jnp.zeros((local, head), jnp.float32))
    before = before * (mine == 0).astype(jnp.float32)

    @pl.loop(1, devices)
    def _(k):
        peer = lax.rem(me + devices - k, devices)
        s_copy(peer, peer).wait_recv()
        r_copy(peer, peer).wait_recv()

    outs = []
    for c in range(kv_count):
        top, total, value = fresh[c]

        def join(i, state):
            top, total, value = state
            other = stat_recv[i, c, 0:1, :]
            both = jnp.maximum(top, other)
            one = jnp.exp2((top - both) * factor)
            two = jnp.exp2((other - both) * factor)
            arrived = res_recv[i, c].astype(jnp.int32).astype(jnp.float32)
            return (
                both,
                total * one + stat_recv[i, c, 1:2, :] * two,
                value * one + arrived * (stat_recv[i, c, 2:3, :] * two),
            )

        if devices <= 4:
            state = (top, total, value)
            for i in range(devices):
                state = join(i, state)
        else:
            state = lax.fori_loop(0, devices, join, (top, total, value))
        outs.append((state[2] / state[1]).T.reshape(steps * local, 1, group, head))
    attended = jnp.concatenate(outs, axis=1) if kv_count > 1 else outs[0]
    attended = attended.reshape(steps * local * all_heads, head).astype(jnp.bfloat16)
    att_ref[...] = attended
    last = att_ref[pl.ds((steps - 1) * local * all_heads, local * all_heads), :].astype(jnp.float32)
    last = last.reshape(local, all_heads, head) * vec_ref[...][None]
    twist = jnp.sum(last, axis=1) - before
    tens_own[...] = twist
    tens_all[mine] = twist

    def t_copy(peer, slot):
        return remote(tens_own, tens_all.at[slot], t_ssem.at[peer], t_rsem.at[slot], tensor=peer)

    def d_copy(peer, slot):
        return remote(dp_own, dp_all.at[slot], d_ssem.at[peer], d_rsem.at[slot], dp=peer)

    @pl.loop(1, tensors)
    def _(k):
        t_copy(lax.rem(mine + k, tensors), mine).start()

    @pl.loop(1, tensors)
    def _(k):
        peer = lax.rem(mine + k, tensors)
        t_copy(peer, peer).wait_recv()

    raw = jnp.sum(tens_all[...], axis=0)
    raw = jnp.broadcast_to(jnp.sum(raw, axis=1, keepdims=True), (local, head))
    dp_own[...] = raw
    dp_all[me] = raw

    @pl.loop(1, devices)
    def _(k):
        d_copy(lax.rem(me + k, devices), me).start()

    @pl.loop(1, devices)
    def _(k):
        peer = lax.rem(me + k, devices)
        d_copy(peer, peer).wait_recv()

    every = dp_all[...]
    largest = jnp.max(jnp.max(every, axis=0), axis=0, keepdims=True)
    mass = jnp.sum(jnp.sum(jnp.exp(every - largest[None]), axis=0), axis=0, keepdims=True)
    logs = raw - (largest + jnp.log(mass))
    flat = jnp.sum(jnp.where(sub8 == lane8, logs, 0.0), axis=0, keepdims=True)
    lw_ref[...] = flat[:, :local]

    @pl.loop(1, devices)
    def _(k):
        peer = lax.rem(me + k, devices)
        m_copy(peer, me).wait_send()
        q_copy(peer, me).wait_send()
        s_copy(peer, me).wait_send()
        r_copy(peer, me).wait_send()
        d_copy(peer, me).wait_send()

    @pl.loop(1, tensors)
    def _(k):
        t_copy(lax.rem(mine + k, tensors), mine).wait_send()


def per_device(devices, tensors, prompt_kv, gen_kv, queries, new_kv, ancestors, prior_twist, twist_vec):
    steps, local, heads, head = queries.shape
    kv_count = prompt_kv.shape[2]
    group = heads // kv_count
    positions = prompt_kv.shape[1]
    cached = gen_kv.shape[2]
    rows = steps * local * group
    sizes = (devices, tensors, steps, local, kv_count, group, positions, cached, head)
    bf16, f32 = jnp.bfloat16, jnp.float32
    vmem = pl.BlockSpec(memory_space=pltpu.VMEM)
    smem = pl.BlockSpec(memory_space=pltpu.SMEM)
    hbm = pl.BlockSpec(memory_space=pl.ANY)
    dma = pltpu.SemaphoreType.DMA
    attended, log_weights = pl.pallas_call(
        functools.partial(kernel, sizes),
        name="decode",
        out_shape=(
            jax.ShapeDtypeStruct((steps * local * heads, head), bf16),
            jax.ShapeDtypeStruct((1, local), f32),
        ),
        in_specs=[smem, smem, vmem, vmem, hbm, hbm, hbm],
        out_specs=(vmem, vmem),
        scratch_shapes=[
            pltpu.VMEM((2, positions * kv_count, head), bf16),
            pltpu.VMEM((local, 2, cached * kv_count, head), bf16),
            pltpu.VMEM((cached * kv_count, head), f32),
            pltpu.VMEM((kv_count, positions, head), bf16),
            pltpu.VMEM((kv_count, head, positions), bf16),
            pltpu.VMEM((kv_count, local * cached, head), bf16),
            pltpu.VMEM((kv_count, head, local * cached), bf16),
            pltpu.VMEM((devices, steps * local * heads, head), bf16),
            pltpu.VMEM((8, rows), f32),
            pltpu.VMEM((devices, 8, rows), f32),
            pltpu.VMEM((devices, kv_count, head, rows), jnp.int16),
            pltpu.VMEM((devices, kv_count, head, rows), jnp.int16),
            pltpu.VMEM((devices, kv_count, 8, rows), f32),
            pltpu.VMEM((devices, kv_count, 8, rows), f32),
            pltpu.VMEM((local, head), f32),
            pltpu.VMEM((tensors, local, head), f32),
            pltpu.VMEM((local, head), f32),
            pltpu.VMEM((devices, local, head), f32),
            dma((4,)),
        ]
        + [dma((devices,))] * 8
        + [dma((tensors,))] * 2
        + [dma((devices,))] * 2,
        compiler_params=pltpu.CompilerParams(
            collective_id=0, has_side_effects=True, vmem_limit_bytes=56 * 1024 * 1024
        ),
    )(
        ancestors,
        prior_twist,
        twist_vec,
        new_kv.reshape(steps, 2, local * kv_count, head),
        queries.reshape(steps * local * heads, head),
        prompt_kv.reshape(2, positions * kv_count, head),
        gen_kv.reshape(local, 2, cached * kv_count, head),
    )
    return (attended.reshape(queries.shape), log_weights.reshape(local))


def solution(mesh):
    placed = (
        P(None, ("parts", "dp"), "tensor", None),
        P(("parts", "dp"), None, None, "tensor", None),
        P(None, ("parts", "dp"), "tensor", None),
        P(None, None, ("parts", "dp"), "tensor", None),
        P(("parts", "dp")),
        P(("parts", "dp")),
        P("tensor", None),
    )
    return jax.shard_map(
        functools.partial(per_device, mesh.shape["dp"], mesh.shape["tensor"]),
        mesh=mesh,
        in_specs=placed,
        out_specs=(P(None, ("parts", "dp"), "tensor", None), P(("parts", "dp"))),
        check_vma=False,
    )
```

```python
import functools
import math

import jax
import jax.numpy as jnp
from jax import lax
from jax.experimental import pallas as pl
from jax.experimental.pallas import tpu as pltpu
from jax.sharding import PartitionSpec as P

MESH = pl.DeviceIdType.MESH
MASKED = -1e30
LEVELS = 32767.0
LOWEST = -3e38


def nt(a, b):
    return lax.dot_general(a, b, (((1,), (1,)), ((), ())), preferred_element_type=jnp.float32)


def tn_dot(a, b):
    return lax.dot_general(a, b, (((0,), (0,)), ((), ())), preferred_element_type=jnp.float32)


def kernel(
    sizes,
    anc_hbm,
    prior_hbm,
    vec_hbm,
    new_hbm,
    q_hbm,
    prompt_hbm,
    gen_hbm,
    att_ref,
    lw_ref,
    anc_ref,
    prior_ref,
    vec_ref,
    new_ref,
    prompt_buf,
    gen_buf,
    wide,
    keys,
    vals,
    gkeys,
    gvals,
    q_all,
    meta_own,
    meta_all,
    res_send,
    res_recv,
    stat_send,
    stat_recv,
    twist_own,
    twist_all,
    local_sem,
    q_ssem,
    q_rsem,
    m_ssem,
    m_rsem,
    r_ssem,
    r_rsem,
    s_ssem,
    s_rsem,
    t_ssem,
    t_rsem,
):
    devices, tensors, steps, local, kv_count, group, positions, cached, head = sizes
    rows = steps * local * group
    all_heads = kv_count * group
    me = lax.axis_index("dp")
    mine = lax.axis_index("tensor")
    factor = math.log2(math.e) / math.sqrt(head)

    def remote(src, dst, ssem, rsem, **where):
        return pltpu.make_async_remote_copy(
            src_ref=src, dst_ref=dst, send_sem=ssem, recv_sem=rsem,
            device_id=where, device_id_type=MESH,
        )

    barrier = pltpu.get_barrier_semaphore()

    @pl.loop(1, devices)
    def _(k):
        pl.semaphore_signal(
            barrier, inc=1, device_id={"dp": lax.rem(me + k, devices)}, device_id_type=MESH
        )

    @pl.loop(1, tensors)
    def _(k):
        pl.semaphore_signal(
            barrier, inc=1, device_id={"tensor": lax.rem(mine + k, tensors)}, device_id_type=MESH
        )

    small = [
        pltpu.make_async_copy(src, dst, local_sem.at[4 + i])
        for i, (src, dst) in enumerate(
            [(anc_hbm, anc_ref), (prior_hbm, prior_ref), (vec_hbm, vec_ref), (new_hbm, new_ref)]
        )
    ]
    for copy in small:
        copy.start()
    copy_q = pltpu.make_async_copy(q_hbm, q_all.at[me], local_sem.at[0])
    copy_q.start()
    copy_k = pltpu.make_async_copy(prompt_hbm.at[0], prompt_buf.at[0], local_sem.at[1])
    copy_k.start()
    copy_v = pltpu.make_async_copy(prompt_hbm.at[1], prompt_buf.at[1], local_sem.at[2])
    copy_v.start()
    copy_g = pltpu.make_async_copy(gen_hbm, gen_buf, local_sem.at[3])
    copy_g.start()

    lane = lax.broadcasted_iota(jnp.int32, (8, rows), 1)
    sub = lax.broadcasted_iota(jnp.int32, (8, rows), 0)
    lane_particle = lax.rem(lax.div(lane, group), local)
    small[0].wait()
    small[1].wait()
    meta = jnp.zeros((8, rows), jnp.float32)
    for j in range(local):
        meta = jnp.where(
            (sub == 0) & (lane_particle == j), anc_ref[j].astype(jnp.float32), meta
        )
        meta = jnp.where((sub == 1) & (lane == j), prior_ref[j], meta)
    meta_own[...] = meta
    meta_all[me] = meta

    pl.semaphore_wait(barrier, devices - 1 + tensors - 1)

    def q_copy(peer, slot):
        return remote(q_hbm, q_all.at[slot], q_ssem.at[peer], q_rsem.at[slot], dp=peer)

    def m_copy(peer, slot):
        return remote(meta_own, meta_all.at[slot], m_ssem.at[peer], m_rsem.at[slot], dp=peer)

    def r_copy(peer, slot):
        return remote(res_send.at[peer], res_recv.at[slot], r_ssem.at[peer], r_rsem.at[slot], dp=peer)

    def s_copy(peer, slot):
        return remote(stat_send.at[peer], stat_recv.at[slot], s_ssem.at[peer], s_rsem.at[slot], dp=peer)

    @pl.loop(1, devices)
    def _(k):
        peer = lax.rem(me + k, devices)
        m_copy(peer, me).start()
        q_copy(peer, me).start()

    def split(source, count):
        wide[pl.ds(0, count * kv_count), :] = source.astype(jnp.float32)
        return [
            wide[pl.ds(c, count, stride=kv_count), :] if kv_count > 1 else wide[pl.ds(0, count), :]
            for c in range(kv_count)
        ]

    chunk = cached

    copy_k.wait()

    @pl.loop(0, positions // chunk)
    def _(i):
        at = pl.ds(pl.multiple_of(i * (chunk * kv_count), chunk * kv_count), chunk * kv_count)
        for c, part in enumerate(split(prompt_buf[0, at, :], chunk)):
            keys[c, pl.ds(pl.multiple_of(i * chunk, chunk), chunk), :] = part.astype(jnp.bfloat16)

    copy_v.wait()

    @pl.loop(0, positions // chunk)
    def _(i):
        at = pl.ds(pl.multiple_of(i * (chunk * kv_count), chunk * kv_count), chunk * kv_count)
        for c, part in enumerate(split(prompt_buf[1, at, :], chunk)):
            vals[c, :, pl.ds(pl.multiple_of(i * chunk, chunk), chunk)] = part.T.astype(jnp.bfloat16)

    copy_g.wait()

    @pl.loop(0, local)
    def _(i):
        at = pl.ds(pl.multiple_of(i * chunk, chunk), chunk)
        for c, part in enumerate(split(gen_buf[i, 0], chunk)):
            gkeys[c, at, :] = part.astype(jnp.bfloat16)
        for c, part in enumerate(split(gen_buf[i, 1], chunk)):
            gvals[c, :, at] = part.T.astype(jnp.bfloat16)

    def rows_of(slot, c):
        q = q_all[slot].astype(jnp.float32).reshape(steps * local, kv_count, group, head)
        return q[:, c].reshape(rows, head).astype(jnp.bfloat16)

    def partial(slot, res, stat):
        ancestor = meta_all[slot, 0:1, :]
        held = (ancestor - (me * local).astype(jnp.float32)).astype(jnp.int32)
        for c in range(kv_count):
            q = rows_of(slot, c)
            score = nt(keys[c], q)
            top = jnp.max(score, axis=0, keepdims=True)
            weight = jnp.exp2((score - top) * factor)
            total = jnp.sum(weight, axis=0, keepdims=True)
            value = jnp.dot(vals[c], weight.astype(jnp.bfloat16), preferred_element_type=jnp.float32)
            gscore = nt(gkeys[c], q).reshape(local, cached, rows)
            which = lax.broadcasted_iota(jnp.int32, (local, 1, rows), 0)
            gscore = jnp.where(which == held[None], gscore, MASKED).reshape(local * cached, rows)
            gtop = jnp.max(gscore, axis=0, keepdims=True)
            gweight = jnp.exp2((gscore - gtop) * factor)
            gtotal = jnp.sum(gweight, axis=0, keepdims=True)
            gvalue = jnp.dot(gvals[c], gweight.astype(jnp.bfloat16), preferred_element_type=jnp.float32)
            both = jnp.maximum(top, gtop)
            one = jnp.exp2((top - both) * factor)
            two = jnp.exp2((gtop - both) * factor)
            value = value * one + gvalue * two
            total = total * one + gtotal * two
            largest = jnp.maximum(jnp.max(jnp.abs(value), axis=0, keepdims=True), 1e-30)
            coded = value * (LEVELS / largest)
            coded = coded + jnp.where(coded >= 0, 0.5, -0.5)
            res[c] = coded.astype(jnp.int32).astype(jnp.int16)
            stat[3 * c : 3 * c + 1, :] = both
            stat[3 * c + 1 : 3 * c + 2, :] = total
            stat[3 * c + 2 : 3 * c + 3, :] = largest * (1.0 / LEVELS)

    copy_q.wait()
    partial(me, res_recv.at[me], stat_recv.at[me])

    @pl.loop(1, devices)
    def _(k):
        peer = lax.rem(me + devices - k, devices)
        m_copy(peer, peer).wait_recv()
        q_copy(peer, peer).wait_recv()
        partial(peer, res_send.at[peer], stat_send.at[peer])
        s_copy(peer, me).start()
        r_copy(peer, me).start()

    small[2].wait()
    small[3].wait()

    fresh_keys = jnp.concatenate(
        [new_ref[t, 0].astype(jnp.float32) for t in range(steps)], axis=0
    ).astype(jnp.bfloat16)
    fresh_vals = jnp.concatenate(
        [new_ref[t, 1].astype(jnp.float32) for t in range(steps)], axis=0
    ).astype(jnp.bfloat16)
    count = steps * local * kv_count
    key_place = lax.broadcasted_iota(jnp.int32, (count, rows), 0)
    row_place = lax.broadcasted_iota(jnp.int32, (count, rows), 1)
    key_head = lax.rem(key_place, kv_count)
    key_particle = lax.rem(lax.div(key_place, kv_count), local)
    key_step = lax.div(key_place, kv_count * local)
    row_particle = lax.rem(lax.div(row_place, group), local)
    row_step = lax.div(row_place, group * local)
    fits = (key_particle == row_particle) & (key_step <= row_step)
    fresh = []
    for c in range(kv_count):
        score = jnp.where(fits & (key_head == c), nt(fresh_keys, rows_of(me, c)), MASKED)
        top = jnp.max(score, axis=0, keepdims=True)
        weight = jnp.exp2((score - top) * factor)
        total = jnp.sum(weight, axis=0, keepdims=True)
        fresh.append((top, total, tn_dot(fresh_vals, weight.astype(jnp.bfloat16))))

    lane8 = lax.broadcasted_iota(jnp.int32, (local, head), 1)
    sub8 = lax.broadcasted_iota(jnp.int32, (local, head), 0)
    own_ancestor = jnp.zeros((local, head), jnp.int32)
    for j in range(local):
        own_ancestor = jnp.where(sub8 == j, anc_ref[j], own_ancestor)

    def add_before(i, before):
        prior = meta_all[i, 1:2, :]
        hit = (own_ancestor - i * local == lane8) & (lane8 < local)
        return before + jnp.where(hit, prior, 0.0)

    before = lax.fori_loop(0, devices, add_before, jnp.zeros((local, head), jnp.float32))
    before = before * (mine == 0).astype(jnp.float32)

    @pl.loop(1, devices)
    def _(k):
        peer = lax.rem(me + devices - k, devices)
        s_copy(peer, peer).wait_recv()
        r_copy(peer, peer).wait_recv()

    outs = []
    for c in range(kv_count):
        top, total, value = fresh[c]

        def join(i, state):
            top, total, value = state
            other = stat_recv[i, 3 * c : 3 * c + 1, :]
            both = jnp.maximum(top, other)
            one = jnp.exp2((top - both) * factor)
            two = jnp.exp2((other - both) * factor)
            arrived = res_recv[i, c].astype(jnp.int32).astype(jnp.float32)
            return (
                both,
                total * one + stat_recv[i, 3 * c + 1 : 3 * c + 2, :] * two,
                value * one + arrived * (stat_recv[i, 3 * c + 2 : 3 * c + 3, :] * two),
            )

        if devices <= 4:
            state = (top, total, value)
            for i in range(devices):
                state = join(i, state)
        else:
            state = lax.fori_loop(0, devices, join, (top, total, value))
        outs.append((state[2] / state[1]).T.reshape(steps * local, 1, group, head))
    attended = jnp.concatenate(outs, axis=1) if kv_count > 1 else outs[0]
    attended = attended.reshape(steps * local * all_heads, head).astype(jnp.bfloat16)
    att_ref[...] = attended
    last = att_ref[pl.ds((steps - 1) * local * all_heads, local * all_heads), :].astype(jnp.float32)
    last = last.reshape(local, all_heads, head) * vec_ref[...][None]
    twist = jnp.sum(last, axis=1) - before
    column = jnp.sum(twist, axis=1, keepdims=True)
    flat = jnp.sum(jnp.where(sub8 == lane8, column, 0.0), axis=0, keepdims=True)
    place = me * tensors + mine
    everyone = devices * tensors
    twist_own[...] = flat
    twist_all[place] = flat

    def t_copy(k, slot):
        peer = lax.rem(place + k, everyone)
        where = dict(dp=lax.div(peer, tensors), tensor=lax.rem(peer, tensors))
        slot = place if slot is None else peer
        return remote(twist_own, twist_all.at[slot], t_ssem.at[peer], t_rsem.at[slot], **where)

    @pl.loop(1, everyone)
    def _(k):
        t_copy(k, None).start()

    @pl.loop(1, everyone)
    def _(k):
        t_copy(k, k).wait_recv()

    def of_device(i):
        return jnp.sum(twist_all[pl.ds(i * tensors, tensors)], axis=0)

    real = lax.broadcasted_iota(jnp.int32, (1, head), 1) < local

    def larger(i, top):
        return jnp.maximum(top, jnp.where(real, of_device(i), LOWEST))

    def heavier(i, mass):
        return mass + jnp.where(real, jnp.exp(of_device(i) - largest), 0.0)

    largest = lax.fori_loop(0, devices, larger, jnp.full((1, head), LOWEST), unroll=devices <= 4)
    largest = jnp.max(largest, axis=1, keepdims=True)
    mass = lax.fori_loop(0, devices, heavier, jnp.zeros((1, head)), unroll=devices <= 4)
    mass = jnp.sum(mass, axis=1, keepdims=True)
    logs = of_device(me) - (largest + jnp.log(mass))
    lw_ref[...] = logs[:, :local]

    @pl.loop(1, devices)
    def _(k):
        peer = lax.rem(me + k, devices)
        m_copy(peer, me).wait_send()
        q_copy(peer, me).wait_send()
        s_copy(peer, me).wait_send()
        r_copy(peer, me).wait_send()

    @pl.loop(1, everyone)
    def _(k):
        t_copy(k, None).wait_send()


def write_out(att_ref, lw_ref, att_out, lw_out, sems):
    copies = [
        pltpu.make_async_copy(att_ref, att_out, sems.at[0]),
        pltpu.make_async_copy(lw_ref, lw_out, sems.at[1]),
    ]
    for copy in copies:
        copy.start()
    for copy in copies:
        copy.wait()


def per_device(devices, tensors, prompt_kv, gen_kv, queries, new_kv, ancestors, prior_twist, twist_vec):
    steps, local, heads, head = queries.shape
    kv_count = prompt_kv.shape[2]
    group = heads // kv_count
    positions = prompt_kv.shape[1]
    cached = gen_kv.shape[2]
    rows = steps * local * group
    stats = 8 * pl.cdiv(3 * kv_count, 8)
    sizes = (devices, tensors, steps, local, kv_count, group, positions, cached, head)
    bf16, f32 = jnp.bfloat16, jnp.float32
    vmem = pl.BlockSpec(memory_space=pltpu.VMEM)
    hbm = pl.BlockSpec(memory_space=pl.ANY)
    dma = pltpu.SemaphoreType.DMA
    attended, log_weights = pl.pallas_call(
        functools.partial(kernel, sizes),
        name="decode",
        out_shape=(
            pltpu.VMEM((steps * local * heads, head), bf16),
            pltpu.VMEM((1, local), f32),
        ),
        in_specs=[hbm] * 7,
        out_specs=(vmem, vmem),
        scratch_shapes=[
            pltpu.SMEM((local,), jnp.int32),
            pltpu.SMEM((local,), f32),
            pltpu.VMEM((heads, head), f32),
            pltpu.VMEM((steps, 2, local * kv_count, head), bf16),
            pltpu.VMEM((2, positions * kv_count, head), bf16),
            pltpu.VMEM((local, 2, cached * kv_count, head), bf16),
            pltpu.VMEM((cached * kv_count, head), f32),
            pltpu.VMEM((kv_count, positions, head), bf16),
            pltpu.VMEM((kv_count, head, positions), bf16),
            pltpu.VMEM((kv_count, local * cached, head), bf16),
            pltpu.VMEM((kv_count, head, local * cached), bf16),
            pltpu.VMEM((devices, steps * local * heads, head), bf16),
            pltpu.VMEM((8, rows), f32),
            pltpu.VMEM((devices, 8, rows), f32),
            pltpu.VMEM((devices, kv_count, head, rows), jnp.int16),
            pltpu.VMEM((devices, kv_count, head, rows), jnp.int16),
            pltpu.VMEM((devices, stats, rows), f32),
            pltpu.VMEM((devices, stats, rows), f32),
            pltpu.VMEM((1, head), f32),
            pltpu.VMEM((devices * tensors, 1, head), f32),
            dma((8,)),
        ]
        + [dma((devices,))] * 8
        + [dma((devices * tensors,))] * 2,
        compiler_params=pltpu.CompilerParams(
            collective_id=0, has_side_effects=True, vmem_limit_bytes=56 * 1024 * 1024
        ),
    )(
        ancestors,
        prior_twist,
        twist_vec,
        new_kv.reshape(steps, 2, local * kv_count, head),
        queries.reshape(steps * local * heads, head),
        prompt_kv.reshape(2, positions * kv_count, head),
        gen_kv.reshape(local, 2, cached * kv_count, head),
    )
    attended, log_weights = pl.pallas_call(
        write_out,
        name="write_out",
        out_shape=(
            jax.ShapeDtypeStruct((steps * local * heads, head), bf16),
            jax.ShapeDtypeStruct((1, local), f32),
        ),
        in_specs=[vmem, vmem],
        out_specs=(hbm, hbm),
        scratch_shapes=[dma((2,))],
    )(pltpu.with_memory_space_constraint(attended, pltpu.VMEM), pltpu.with_memory_space_constraint(log_weights, pltpu.VMEM))
    return (attended.reshape(queries.shape), log_weights.reshape(local))


def solution(mesh):
    placed = (
        P(None, ("parts", "dp"), "tensor", None),
        P(("parts", "dp"), None, None, "tensor", None),
        P(None, ("parts", "dp"), "tensor", None),
        P(None, None, ("parts", "dp"), "tensor", None),
        P(("parts", "dp")),
        P(("parts", "dp")),
        P("tensor", None),
    )
    return jax.shard_map(
        functools.partial(per_device, mesh.shape["dp"], mesh.shape["tensor"]),
        mesh=mesh,
        in_specs=placed,
        out_specs=(P(None, ("parts", "dp"), "tensor", None), P(("parts", "dp"))),
        check_vma=False,
    )
```

```python
import functools
import math

import jax
import jax.numpy as jnp
from jax import lax
from jax.experimental import pallas as pl
from jax.experimental.pallas import tpu as pltpu
from jax.sharding import PartitionSpec as P

MESH = pl.DeviceIdType.MESH
MASKED = -1e30
LEVELS = 32767.0
LOWEST = -3e38


def nt(a, b):
    return lax.dot_general(a, b, (((1,), (1,)), ((), ())), preferred_element_type=jnp.float32)


def tn_dot(a, b):
    return lax.dot_general(a, b, (((0,), (0,)), ((), ())), preferred_element_type=jnp.float32)


def kernel(
    sizes,
    anc_hbm,
    prior_hbm,
    vec_hbm,
    new_hbm,
    q_hbm,
    prompt_hbm,
    gen_hbm,
    att_ref,
    lw_ref,
    anc_ref,
    prior_ref,
    vec_ref,
    new_ref,
    prompt_buf,
    gen_buf,
    wide,
    keys,
    vals,
    gkeys,
    gvals,
    q_all,
    meta_own,
    meta_all,
    res_send,
    res_recv,
    stat_send,
    stat_recv,
    twist_own,
    twist_all,
    local_sem,
    q_ssem,
    q_rsem,
    m_ssem,
    m_rsem,
    r_ssem,
    r_rsem,
    s_ssem,
    s_rsem,
    t_ssem,
    t_rsem,
):
    devices, tensors, steps, local, kv_count, group, positions, cached, head = sizes
    rows = steps * local * group
    all_heads = kv_count * group
    me = lax.axis_index("dp")
    mine = lax.axis_index("tensor")
    factor = math.log2(math.e) / math.sqrt(head)

    def over(stop):
        def run(body):
            if stop > 16:
                pl.loop(1, stop)(body)
            else:
                for k in range(1, stop):
                    body(k)

        return run

    def remote(src, dst, ssem, rsem, **where):
        return pltpu.make_async_remote_copy(
            src_ref=src, dst_ref=dst, send_sem=ssem, recv_sem=rsem,
            device_id=where, device_id_type=MESH,
        )

    barrier = pltpu.get_barrier_semaphore()

    @over(devices)
    def _(k):
        pl.semaphore_signal(
            barrier, inc=1, device_id={"dp": lax.rem(me + k, devices)}, device_id_type=MESH
        )

    @over(tensors)
    def _(k):
        pl.semaphore_signal(
            barrier, inc=1, device_id={"tensor": lax.rem(mine + k, tensors)}, device_id_type=MESH
        )

    small = [
        pltpu.make_async_copy(src, dst, local_sem.at[4 + i])
        for i, (src, dst) in enumerate(
            [(anc_hbm, anc_ref), (prior_hbm, prior_ref), (vec_hbm, vec_ref), (new_hbm, new_ref)]
        )
    ]
    for copy in small:
        copy.start()
    copy_q = pltpu.make_async_copy(q_hbm, q_all.at[me], local_sem.at[0])
    copy_q.start()
    copy_k = pltpu.make_async_copy(prompt_hbm.at[0], prompt_buf.at[0], local_sem.at[1])
    copy_k.start()
    copy_v = pltpu.make_async_copy(prompt_hbm.at[1], prompt_buf.at[1], local_sem.at[2])
    copy_v.start()
    copy_g = pltpu.make_async_copy(gen_hbm, gen_buf, local_sem.at[3])
    copy_g.start()

    lane = lax.broadcasted_iota(jnp.int32, (8, rows), 1)
    sub = lax.broadcasted_iota(jnp.int32, (8, rows), 0)
    lane_particle = lax.rem(lax.div(lane, group), local)
    small[0].wait()
    small[1].wait()
    meta = jnp.zeros((8, rows), jnp.float32)
    for j in range(local):
        meta = jnp.where(
            (sub == 0) & (lane_particle == j), anc_ref[j].astype(jnp.float32), meta
        )
        meta = jnp.where((sub == 1) & (lane == j), prior_ref[j], meta)
    meta_own[...] = meta
    meta_all[me] = meta

    pl.semaphore_wait(barrier, devices - 1 + tensors - 1)

    def q_copy(peer, slot):
        return remote(q_hbm, q_all.at[slot], q_ssem.at[peer], q_rsem.at[slot], dp=peer)

    def m_copy(peer, slot):
        return remote(meta_own, meta_all.at[slot], m_ssem.at[peer], m_rsem.at[slot], dp=peer)

    def r_copy(peer, slot):
        return remote(res_send.at[peer], res_recv.at[slot], r_ssem.at[peer], r_rsem.at[slot], dp=peer)

    def s_copy(peer, slot):
        return remote(stat_send.at[peer], stat_recv.at[slot], s_ssem.at[peer], s_rsem.at[slot], dp=peer)

    @over(devices)
    def _(k):
        peer = lax.rem(me + k, devices)
        m_copy(peer, me).start()
        q_copy(peer, me).start()

    def split(source, count):
        wide[pl.ds(0, count * kv_count), :] = source.astype(jnp.float32)
        return [
            wide[pl.ds(c, count, stride=kv_count), :] if kv_count > 1 else wide[pl.ds(0, count), :]
            for c in range(kv_count)
        ]

    chunk = cached

    copy_k.wait()

    @pl.loop(0, positions // chunk)
    def _(i):
        at = pl.ds(pl.multiple_of(i * (chunk * kv_count), chunk * kv_count), chunk * kv_count)
        for c, part in enumerate(split(prompt_buf[0, at, :], chunk)):
            place = pl.ds(pl.multiple_of(i * chunk, chunk), chunk)
            keys[place, c * head : (c + 1) * head] = part.astype(jnp.bfloat16)

    copy_v.wait()

    @pl.loop(0, positions // chunk)
    def _(i):
        at = pl.ds(pl.multiple_of(i * (chunk * kv_count), chunk * kv_count), chunk * kv_count)
        for c, part in enumerate(split(prompt_buf[1, at, :], chunk)):
            vals[c, :, pl.ds(pl.multiple_of(i * chunk, chunk), chunk)] = part.T.astype(jnp.bfloat16)

    copy_g.wait()

    @pl.loop(0, local)
    def _(i):
        at = pl.ds(pl.multiple_of(i * chunk, chunk), chunk)
        for c, part in enumerate(split(gen_buf[i, 0], chunk)):
            gkeys[at, c * head : (c + 1) * head] = part.astype(jnp.bfloat16)
        for c, part in enumerate(split(gen_buf[i, 1], chunk)):
            gvals[c, :, at] = part.T.astype(jnp.bfloat16)

    def rows_of(slot, c):
        q = q_all[slot].astype(jnp.float32).reshape(steps * local, kv_count, group, head)
        return q[:, c].reshape(rows, head).astype(jnp.bfloat16)

    def partial(slot, res, stat):
        ancestor = meta_all[slot, 0:1, :]
        held = (ancestor - (me * local).astype(jnp.float32)).astype(jnp.int32)
        each = [rows_of(slot, c) for c in range(kv_count)]
        blank = jnp.zeros((rows, head), jnp.bfloat16)
        q = jnp.concatenate(
            [
                jnp.concatenate([each[c] if c == b else blank for b in range(kv_count)], axis=1)
                for c in range(kv_count)
            ],
            axis=0,
        )
        held = jnp.concatenate([held] * kv_count, axis=1)
        score = nt(keys[...], q)
        tops = jnp.max(score, axis=0, keepdims=True)
        weight = jnp.exp2((score - tops) * factor)
        totals = jnp.sum(weight, axis=0, keepdims=True)
        weight = weight.astype(jnp.bfloat16)
        gscore = nt(gkeys[...], q).reshape(local, cached, kv_count * rows)
        which = lax.broadcasted_iota(jnp.int32, (local, 1, kv_count * rows), 0)
        gscore = jnp.where(which == held[None], gscore, MASKED)
        gscore = gscore.reshape(local * cached, kv_count * rows)
        gtops = jnp.max(gscore, axis=0, keepdims=True)
        gweight = jnp.exp2((gscore - gtops) * factor)
        gtotals = jnp.sum(gweight, axis=0, keepdims=True)
        gweight = gweight.astype(jnp.bfloat16)
        for c in range(kv_count):
            span = slice(c * rows, (c + 1) * rows)
            top, total, gtop, gtotal = tops[:, span], totals[:, span], gtops[:, span], gtotals[:, span]
            value = jnp.dot(vals[c], weight[:, span], preferred_element_type=jnp.float32)
            gvalue = jnp.dot(gvals[c], gweight[:, span], preferred_element_type=jnp.float32)
            both = jnp.maximum(top, gtop)
            one = jnp.exp2((top - both) * factor)
            two = jnp.exp2((gtop - both) * factor)
            value = value * one + gvalue * two
            total = total * one + gtotal * two
            largest = jnp.maximum(jnp.max(jnp.abs(value), axis=0, keepdims=True), 1e-30)
            coded = value * (LEVELS / largest)
            coded = coded + jnp.where(coded >= 0, 0.5, -0.5)
            res[c] = coded.astype(jnp.int32).astype(jnp.int16)
            stat[3 * c : 3 * c + 1, :] = both
            stat[3 * c + 1 : 3 * c + 2, :] = total
            stat[3 * c + 2 : 3 * c + 3, :] = largest * (1.0 / LEVELS)

    copy_q.wait()
    partial(me, res_recv.at[me], stat_recv.at[me])

    @pl.loop(1, devices)
    def _(k):
        peer = lax.rem(me + devices - k, devices)
        m_copy(peer, peer).wait_recv()
        q_copy(peer, peer).wait_recv()
        partial(peer, res_send.at[peer], stat_send.at[peer])
        s_copy(peer, me).start()
        r_copy(peer, me).start()

    small[2].wait()
    small[3].wait()

    fresh_keys = jnp.concatenate(
        [new_ref[t, 0].astype(jnp.float32) for t in range(steps)], axis=0
    ).astype(jnp.bfloat16)
    fresh_vals = jnp.concatenate(
        [new_ref[t, 1].astype(jnp.float32) for t in range(steps)], axis=0
    ).astype(jnp.bfloat16)
    count = steps * local * kv_count
    key_place = lax.broadcasted_iota(jnp.int32, (count, rows), 0)
    row_place = lax.broadcasted_iota(jnp.int32, (count, rows), 1)
    key_head = lax.rem(key_place, kv_count)
    key_particle = lax.rem(lax.div(key_place, kv_count), local)
    key_step = lax.div(key_place, kv_count * local)
    row_particle = lax.rem(lax.div(row_place, group), local)
    row_step = lax.div(row_place, group * local)
    fits = (key_particle == row_particle) & (key_step <= row_step)
    fresh = []
    for c in range(kv_count):
        score = jnp.where(fits & (key_head == c), nt(fresh_keys, rows_of(me, c)), MASKED)
        top = jnp.max(score, axis=0, keepdims=True)
        weight = jnp.exp2((score - top) * factor)
        total = jnp.sum(weight, axis=0, keepdims=True)
        fresh.append((top, total, tn_dot(fresh_vals, weight.astype(jnp.bfloat16))))

    lane8 = lax.broadcasted_iota(jnp.int32, (local, head), 1)
    sub8 = lax.broadcasted_iota(jnp.int32, (local, head), 0)
    own_ancestor = jnp.zeros((local, head), jnp.int32)
    for j in range(local):
        own_ancestor = jnp.where(sub8 == j, anc_ref[j], own_ancestor)

    def add_before(i, before):
        prior = meta_all[i, 1:2, :]
        hit = (own_ancestor - i * local == lane8) & (lane8 < local)
        return before + jnp.where(hit, prior, 0.0)

    before = lax.fori_loop(0, devices, add_before, jnp.zeros((local, head), jnp.float32))
    before = before * (mine == 0).astype(jnp.float32)

    @over(devices)
    def _(k):
        peer = lax.rem(me + devices - k, devices)
        s_copy(peer, peer).wait_recv()
        r_copy(peer, peer).wait_recv()

    outs = []
    for c in range(kv_count):
        top, total, value = fresh[c]

        def join(i, state):
            top, total, value = state
            other = stat_recv[i, 3 * c : 3 * c + 1, :]
            both = jnp.maximum(top, other)
            one = jnp.exp2((top - both) * factor)
            two = jnp.exp2((other - both) * factor)
            arrived = res_recv[i, c].astype(jnp.int32).astype(jnp.float32)
            return (
                both,
                total * one + stat_recv[i, 3 * c + 1 : 3 * c + 2, :] * two,
                value * one + arrived * (stat_recv[i, 3 * c + 2 : 3 * c + 3, :] * two),
            )

        if devices <= 4:
            state = (top, total, value)
            for i in range(devices):
                state = join(i, state)
        else:
            state = lax.fori_loop(0, devices, join, (top, total, value))
        outs.append((state[2] / state[1]).T.reshape(steps * local, 1, group, head))
    attended = jnp.concatenate(outs, axis=1) if kv_count > 1 else outs[0]
    attended = attended.reshape(steps * local * all_heads, head).astype(jnp.bfloat16)
    att_ref[...] = attended
    last = att_ref[pl.ds((steps - 1) * local * all_heads, local * all_heads), :].astype(jnp.float32)
    last = last.reshape(local, all_heads, head) * vec_ref[...][None]
    twist = jnp.sum(last, axis=1) - before
    column = jnp.sum(twist, axis=1, keepdims=True)
    flat = jnp.sum(jnp.where(sub8 == lane8, column, 0.0), axis=0, keepdims=True)
    place = me * tensors + mine
    everyone = devices * tensors
    twist_own[...] = flat
    twist_all[place] = flat

    def t_copy(k, slot):
        peer = lax.rem(place + k, everyone)
        where = dict(dp=lax.div(peer, tensors), tensor=lax.rem(peer, tensors))
        slot = place if slot is None else peer
        return remote(twist_own, twist_all.at[slot], t_ssem.at[peer], t_rsem.at[slot], **where)

    @over(everyone)
    def _(k):
        t_copy(k, None).start()

    @over(everyone)
    def _(k):
        t_copy(k, k).wait_recv()

    def of_device(i):
        return jnp.sum(twist_all[pl.ds(i * tensors, tensors)], axis=0)

    real = lax.broadcasted_iota(jnp.int32, (1, head), 1) < local

    def larger(i, top):
        return jnp.maximum(top, jnp.where(real, of_device(i), LOWEST))

    def heavier(i, mass):
        return mass + jnp.where(real, jnp.exp(of_device(i) - largest), 0.0)

    largest = lax.fori_loop(0, devices, larger, jnp.full((1, head), LOWEST), unroll=devices <= 4)
    largest = jnp.max(largest, axis=1, keepdims=True)
    mass = lax.fori_loop(0, devices, heavier, jnp.zeros((1, head)), unroll=devices <= 4)
    mass = jnp.sum(mass, axis=1, keepdims=True)
    logs = of_device(me) - (largest + jnp.log(mass))
    lw_ref[...] = logs[:, :local]

    @over(devices)
    def _(k):
        peer = lax.rem(me + k, devices)
        m_copy(peer, me).wait_send()
        q_copy(peer, me).wait_send()
        s_copy(peer, me).wait_send()
        r_copy(peer, me).wait_send()

    @over(everyone)
    def _(k):
        t_copy(k, None).wait_send()


def write_out(att_ref, lw_ref, att_out, lw_out, sems):
    copies = [
        pltpu.make_async_copy(att_ref, att_out, sems.at[0]),
        pltpu.make_async_copy(lw_ref, lw_out, sems.at[1]),
    ]
    for copy in copies:
        copy.start()
    for copy in copies:
        copy.wait()


def per_device(devices, tensors, prompt_kv, gen_kv, queries, new_kv, ancestors, prior_twist, twist_vec):
    steps, local, heads, head = queries.shape
    kv_count = prompt_kv.shape[2]
    group = heads // kv_count
    positions = prompt_kv.shape[1]
    cached = gen_kv.shape[2]
    rows = steps * local * group
    stats = 8 * pl.cdiv(3 * kv_count, 8)
    sizes = (devices, tensors, steps, local, kv_count, group, positions, cached, head)
    bf16, f32 = jnp.bfloat16, jnp.float32
    vmem = pl.BlockSpec(memory_space=pltpu.VMEM)
    hbm = pl.BlockSpec(memory_space=pl.ANY)
    dma = pltpu.SemaphoreType.DMA
    attended, log_weights = pl.pallas_call(
        functools.partial(kernel, sizes),
        name="decode",
        out_shape=(
            pltpu.VMEM((steps * local * heads, head), bf16),
            pltpu.VMEM((1, local), f32),
        ),
        in_specs=[hbm] * 7,
        out_specs=(vmem, vmem),
        scratch_shapes=[
            pltpu.SMEM((local,), jnp.int32),
            pltpu.SMEM((local,), f32),
            pltpu.VMEM((heads, head), f32),
            pltpu.VMEM((steps, 2, local * kv_count, head), bf16),
            pltpu.VMEM((2, positions * kv_count, head), bf16),
            pltpu.VMEM((local, 2, cached * kv_count, head), bf16),
            pltpu.VMEM((cached * kv_count, head), f32),
            pltpu.VMEM((positions, kv_count * head), bf16),
            pltpu.VMEM((kv_count, head, positions), bf16),
            pltpu.VMEM((local * cached, kv_count * head), bf16),
            pltpu.VMEM((kv_count, head, local * cached), bf16),
            pltpu.VMEM((devices, steps * local * heads, head), bf16),
            pltpu.VMEM((8, rows), f32),
            pltpu.VMEM((devices, 8, rows), f32),
            pltpu.VMEM((devices, kv_count, head, rows), jnp.int16),
            pltpu.VMEM((devices, kv_count, head, rows), jnp.int16),
            pltpu.VMEM((devices, stats, rows), f32),
            pltpu.VMEM((devices, stats, rows), f32),
            pltpu.VMEM((1, head), f32),
            pltpu.VMEM((devices * tensors, 1, head), f32),
            dma((8,)),
        ]
        + [dma((devices,))] * 8
        + [dma((devices * tensors,))] * 2,
        compiler_params=pltpu.CompilerParams(
            collective_id=0, has_side_effects=True, vmem_limit_bytes=56 * 1024 * 1024
        ),
    )(
        ancestors,
        prior_twist,
        twist_vec,
        new_kv.reshape(steps, 2, local * kv_count, head),
        queries.reshape(steps * local * heads, head),
        prompt_kv.reshape(2, positions * kv_count, head),
        gen_kv.reshape(local, 2, cached * kv_count, head),
    )
    attended, log_weights = pl.pallas_call(
        write_out,
        name="write_out",
        out_shape=(
            jax.ShapeDtypeStruct((steps * local * heads, head), bf16),
            jax.ShapeDtypeStruct((1, local), f32),
        ),
        in_specs=[vmem, vmem],
        out_specs=(hbm, hbm),
        scratch_shapes=[dma((2,))],
    )(pltpu.with_memory_space_constraint(attended, pltpu.VMEM), pltpu.with_memory_space_constraint(log_weights, pltpu.VMEM))
    return (attended.reshape(queries.shape), log_weights.reshape(local))


def solution(mesh):
    placed = (
        P(None, ("parts", "dp"), "tensor", None),
        P(("parts", "dp"), None, None, "tensor", None),
        P(None, ("parts", "dp"), "tensor", None),
        P(None, None, ("parts", "dp"), "tensor", None),
        P(("parts", "dp")),
        P(("parts", "dp")),
        P("tensor", None),
    )
    return jax.shard_map(
        functools.partial(per_device, mesh.shape["dp"], mesh.shape["tensor"]),
        mesh=mesh,
        in_specs=placed,
        out_specs=(P(None, ("parts", "dp"), "tensor", None), P(("parts", "dp"))),
        check_vma=False,
    )
```
